128 devices in a mesh: panel: 4 (over x_lo, core), obs: 32 (over y, z, x_hi).
Axes of the slice: x: 4 (x_hi: 2, x_lo: 2; x = x_hi * 2 + x_lo), y: 4, z: 4, core: 2. Of those that a mesh axis runs over, the one named last changes fastest.
Arguments:
- les_rows: bfloat16 [16384, 2, 128], P(('panel', 'obs')), may hold values from -6 to 6
- les_dest: int32 [16384, 1], P(('panel', 'obs')), may hold values from 0 to 127; in each aligned block of 128 rows (0 to 127, 128 to 255, ...) at most 2 rows name the same one
- loading_weight: bfloat16 [32768, 4096], P('panel', 'obs'), may hold values from -0.046875 to 0.046875
- thickness_weight: bfloat16 [32768, 4096], P('panel', 'obs'), may hold values from -0.046875 to 0.046875
- delays: int32 [64, 32], P('panel', 'obs'), may hold values from 0 to 64
Outputs:
- acoustic_pressure: float32 [128, 4096], P('panel', 'obs')
The draws below stay inside these ranges and needn't reach their ends.
Inputs may be any that keep to these rules, and one draw needn't show every extreme that they name: `les_dest`: in the aligned blocks of 128 rows of one LES owner, no destination is named by more than 2 rows, a bound that some block reaches; every destination is named by some row.
All inputs are finite; a program needn't handle non-finite values.
Results may differ from the reference program's by a relative error of at most 0.0018.
Values may be sent and summed in bfloat16 or wider, within the bound.
A program may use at most 64 MiB of HBM per device.

```python
import math
import jax
import jax.numpy as jnp
import numpy as np
from jax import lax

TS = 128
ROWS_DEV = 128
PBLK = 512
OBLK = 128
DMAX = 64
CAP = 2
SLOTS_DEV = 256
PANELS = 32768
ROWS_TOTAL = 16384
OBSERVERS = 4096
N_PANEL = 4
N_OBS = 32
DEVICES = 128


def place_ends(drawn, key, low, high):
    spot = [jax.random.randint(jax.random.fold_in(key, axis), (), 0, length) for axis, length in enumerate(drawn.shape)]
    longest = drawn.shape.index(max(drawn.shape))
    next_to = spot[:longest] + [(spot[longest] + 1) % drawn.shape[longest]] + spot[longest + 1:]
    return drawn.at[tuple(spot)].set(low).at[tuple(next_to)].set(high)


def steps_of(stream_key, shape, cuts, least, largest):
    level = 1.0
    for position, shards_of in cuts:
        steps = jax.random.uniform(jax.random.fold_in(jax.random.fold_in(stream_key, 6), position), (shards_of,), jnp.float32, least / len(cuts), largest / len(cuts))
        level = level * jnp.repeat(jnp.exp(steps), shape[position] // shards_of).reshape((-1,) + (1,) * (len(shape) - 1 - position))
    return level


def deal_out(key, own, number, rows, number_of, top, reach, lean):
    ranking = jax.random.permutation(key, number_of)
    heavy_load, ordinary = load_shares(number_of, rows * top, reach, lean, True), load_shares(number_of, rows * top, reach, lean, False)
    places = jnp.arange(number_of)

    def named(tallies, rotation):
        used = int((tallies > 0).sum())
        fixed = max(1, used // 4)
        shifted = fixed + (places - fixed + rotation * (used - fixed)) % max(1, number_of - fixed)
        return jnp.zeros((number_of,), jnp.int32).at[ranking[jnp.where(places < fixed, places, shifted)]].set(jnp.asarray(tallies, jnp.int32))

    tallies = jnp.where(number % 4 == 0, named(heavy_load, number // 4), named(ordinary, number - number // 4 - 1))
    mixed = jax.random.permutation(jax.random.fold_in(own, 3), number_of)
    donor, receiver = mixed[0:number_of // 2 * 2:2], mixed[1:number_of // 2 * 2:2]
    room = jnp.minimum(tallies[donor] - 1, reach - tallies[receiver]) // 2
    room = jnp.where((donor == ranking[0]) | (receiver == ranking[0]) | (tallies[receiver] == 0), 0, jnp.maximum(room, 0))
    shifted = jax.random.randint(jax.random.fold_in(own, 4), (number_of // 2,), 0, 1 << 20) % (room + 1)
    tallies = tallies.at[donor].add(-shifted).at[receiver].add(shifted)
    members = jnp.searchsorted(jnp.cumsum(tallies), jnp.arange(rows * top), side="right").astype(jnp.int32)
    table = members.reshape(top, rows).T
    table = table[jax.random.permutation(jax.random.fold_in(own, 1), rows)]
    rotation = jax.random.randint(jax.random.fold_in(own, 2), (rows, 1), 0, top)
    return jnp.take_along_axis(table, (jnp.arange(top)[None, :] + rotation) % top, axis=1)


def load_shares(amount, total, limit, skew, full):
    portions = [(1 << 20) // math.isqrt(standing ** skew) + 1 for standing in range(1, amount + 1)]
    largest = limit if full else min(limit, max(-(-total // amount), total * portions[0] // sum(portions)))
    least = 1 if total - largest >= amount - 1 else 0
    holding, rest = [largest] + [least] * (amount - 1), total - largest - least * (amount - 1)
    while rest > 0:
        candidates = [i for i in range(1, amount) if holding[i] < largest] or [i for i in range(1, amount) if holding[i] < limit]
        mass, left = sum([portions[i] for i in candidates]), rest
        for i in candidates:
            addition = min(limit - holding[i], max(1, left * portions[i] // mass), rest)
            holding[i] = holding[i] + addition
            rest = rest - addition
    return np.array(holding)


def centred(own_key, shape, scale, bound, split=(), kind=jnp.bfloat16):
    drawn = jax.random.normal(own_key, shape, jnp.float32) * scale
    if len(split) > 0:
        drawn = steps_of(own_key, shape, split, -0.22, 0.18) * drawn
    return jnp.clip(drawn, min=-bound, max=bound).astype(kind)


def setup_inputs(seed: int = 0) -> dict:
    seeds = jax.random.split(jax.random.key(seed), 6)
    les_rows = centred(seeds[0], (ROWS_TOTAL, 2, TS), 1.0, 6.0, ((0, 128),))
    les_dest_keys = jax.random.split(jax.random.fold_in(seeds[1], 1), ROWS_TOTAL // ROWS_DEV)
    les_dest_turns = jax.random.permutation(jax.random.fold_in(seeds[1], 3), ROWS_TOTAL // ROWS_DEV)
    les_dest = jax.vmap(lambda own, number: deal_out(jax.random.fold_in(seeds[1], 2), own, number, ROWS_DEV, DEVICES, 1, CAP, 2))(les_dest_keys, les_dest_turns).reshape((ROWS_TOTAL, 1))
    loading_weight = centred(seeds[2], (PANELS, OBSERVERS), (PANELS // 2) ** -0.5, 0.046875, ((0, 4), (1, 32)))
    thickness_weight = centred(seeds[3], (PANELS, OBSERVERS), (PANELS // 2) ** -0.5, 0.046875, ((0, 4), (1, 32)))
    delays = place_ends(jax.random.randint(seeds[4], (PANELS // PBLK, OBSERVERS // OBLK), 0, DMAX + 1), jax.random.fold_in(seeds[4], 1), 0, DMAX).astype(jnp.int32)
    return dict(les_rows=les_rows, les_dest=les_dest, loading_weight=loading_weight, thickness_weight=thickness_weight, delays=delays)


def owner_ranks(dest_block, count):
    onehot = (dest_block[:, :, None] == jnp.arange(count, dtype=jnp.int32)[None, None, :]).astype(jnp.int32)
    earlier = jnp.cumsum(onehot, axis=1) - onehot
    return jnp.sum(earlier * onehot, axis=2).astype(jnp.int32)


def delay_block(block, delay):
    steps = block.shape[0]
    padded = jnp.concatenate([jnp.zeros_like(block), block], axis=0)
    start = (steps - delay).astype(jnp.int32)
    return lax.dynamic_slice_in_dim(padded, start, steps, 0)


def shift_time(values, delay_row):
    steps = values.shape[0]
    blocks = delay_row.shape[0]
    shaped = values.reshape(steps, blocks, -1)
    moved = jax.vmap(delay_block, in_axes=(1, 0), out_axes=1)(shaped, delay_row.astype(jnp.int32))
    return moved.reshape(steps, -1)


def reference(les_rows, les_dest, loading_weight, thickness_weight, delays):
    count = N_PANEL * N_OBS
    dest_block = les_dest[:, 0].astype(jnp.int32).reshape(count, ROWS_DEV)
    rank = owner_ranks(dest_block, count)
    owner = jnp.arange(count, dtype=jnp.int32)[:, None]
    slot = (dest_block * SLOTS_DEV + owner * CAP + rank).reshape(-1)
    surface = jnp.zeros((PANELS, 2, TS), les_rows.dtype).at[slot].set(les_rows)
    velocity = surface[:, 1, :].astype(jnp.float32)
    padded = jnp.pad(velocity, ((0, 0), (1, 1)))
    rate = ((padded[:, 2:] - padded[:, :-2]) * 0.5).astype(jnp.bfloat16)
    pressure_src = surface[:, 0, :]
    nblocks = PANELS // PBLK
    press_blocks = pressure_src.reshape(nblocks, PBLK, TS)
    rate_blocks = rate.reshape(nblocks, PBLK, TS)
    load_blocks = loading_weight.reshape(nblocks, PBLK, OBSERVERS)
    thick_blocks = thickness_weight.reshape(nblocks, PBLK, OBSERVERS)

    def one_block(total, inputs):
        press_b, rate_b, load_b, thick_b, delay_b = inputs
        dims = (((0,), (0,)), ((), ()))
        term = lax.dot_general(press_b, load_b, dims, preferred_element_type=jnp.float32)
        term = term + lax.dot_general(rate_b, thick_b, dims, preferred_element_type=jnp.float32)
        return total + shift_time(term, delay_b), None

    start = jnp.zeros((TS, OBSERVERS), jnp.float32)
    total, unused = lax.scan(one_block, start, (press_blocks, rate_blocks, load_blocks, thick_blocks, delays))
    return total
```

```python
import itertools

import jax
import jax.numpy as jnp
import numpy as np
from jax import lax
from jax.experimental import pallas as pl
from jax.experimental.pallas import tpu as pltpu
from jax.sharding import PartitionSpec as P

MESH = pl.DeviceIdType.MESH
RING = 4
CHIPS = RING**3
CHUNK = 8
CHUNKS = CHIPS // CHUNK
RELAY = 4

HOPS = (0, 1, 2, 1)
OFFSETS = sorted(itertools.product(range(RING), repeat=3), key=lambda o: (sum(HOPS[v] for v in o), o))
PLACE = {offset: n for n, offset in enumerate(OFFSETS)}


def routes(offset):
    found = []
    moved = [i for i in range(3) if offset[i]]
    for axis in range(3):
        others = [i for i in moved if i != axis]
        classes = [k for k in range(3) if all((i - k) % 3 < (axis - k) % 3 for i in others)]
        if not classes:
            continue
        if offset[axis] == 0:
            steps = (1, 3)
        else:
            parity = (axis + sum(offset[i] for i in range(3) if i != axis)) % 2
            turn = 1 if parity == 0 else 3
            steps = (turn,) if offset[axis] == turn else ()
        for step in steps:
            found.append((axis, step, classes))
    return found


EDGES = {}
for _n, _offset in enumerate(OFFSETS):
    for _axis, _step, _classes in routes(_offset):
        EDGES[(_n, _axis, _step)] = len(EDGES)


def wrap(value):
    return lax.rem(value, RING)


def kernel(
    blk_ref, pos_ref, permt_ref, load_ref, thick_ref, delay_ref, out_ref,
    buf, meta, wraw, wperm, wt, onehot, rows_id, sel, shifted, acc, part, arrived,
    edge_sem, recv_sem, relay_send, relay_recv, meta_send, meta_recv, w_sem, own_sem, rs_send, rs_recv,
):
    p = lax.axis_index("panel")
    o = lax.axis_index("obs")
    x_lo, core = p // 2, lax.rem(p, 2)
    y, z, x_hi = o // 8, lax.rem(o // 2, 4), lax.rem(o, 2)
    x = x_hi * 2 + x_lo
    me = (x, y, z)

    def device(cx, cy, cz, cc):
        return (lax.rem(cx, 2) * 2 + cc, cy * 8 + cz * 2 + cx // 2)

    def beside(axis, step):
        there = list(me)
        there[axis] = wrap(me[axis] + step)
        return device(*there, core)

    near = {(axis, step): beside(axis, step) for axis in range(3) for step in (1, 3)}
    partner = device(x, y, z, 1 - core)
    line = [(device(wrap(x + s), y, z, core), s * 2) for s in range(1, 4)]
    line += [(device(wrap(x + s), y, z, 1 - core), s * 2 + 1) for s in range(0, 4)]
    column = [(device(x, y, wrap(z + s), core), s) for s in range(1, 4)]
    plane = [(device(x, wrap(y + s), z, core), s) for s in range(1, 4)]

    for index, source in enumerate((load_ref, thick_ref)):
        pltpu.make_async_copy(source, wraw.at[index], w_sem.at[index]).start()
    own = pltpu.make_async_copy(blk_ref, buf.at[0, 0], own_sem.at[0])
    own.start()
    own_meta = pltpu.make_async_copy(pos_ref, meta.at[y, z, x * 2 + core], own_sem.at[1])
    own_meta.start()

    barrier = pltpu.get_barrier_semaphore()
    for target, unused in line + column + plane:
        pl.semaphore_signal(barrier, inc=1, device_id=target, device_id_type=MESH)
    pl.semaphore_wait(barrier, 13)

    def source_of(n):
        offset = OFFSETS[n]
        return [wrap(me[i] + (RING - offset[i])) for i in range(3)]

    def edges(n, act):
        offset = OFFSETS[n]
        there = source_of(n)
        kind = lax.rem(there[0] + there[1] + there[2] + core, 3)
        for axis, step, classes in routes(offset):
            landed = list(offset)
            landed[axis] = (offset[axis] + step) % RING
            slot = PLACE[tuple(landed)]
            edge = EDGES[(n, axis, step)]
            copy = pltpu.make_async_remote_copy(
                src_ref=blk_ref if n == 0 else buf.at[0, n],
                dst_ref=buf.at[0, slot],
                send_sem=edge_sem.at[edge],
                recv_sem=recv_sem.at[slot],
                device_id=near[(axis, step)],
                device_id_type=MESH,
            )
            if len(classes) == 3:
                act(copy)
            else:
                test = kind == classes[0]
                for k in classes[1:]:
                    test = jnp.logical_or(test, kind == k)

                @pl.when(test)
                def _():
                    act(copy)

    def arrival(n):
        return pltpu.make_async_remote_copy(
            src_ref=blk_ref, dst_ref=buf.at[0, n], send_sem=edge_sem.at[0], recv_sem=recv_sem.at[n],
            device_id=partner, device_id_type=MESH,
        )

    def relay(group):
        span = pl.ds(group * RELAY, RELAY)
        return pltpu.make_async_remote_copy(
            src_ref=buf.at[0, span], dst_ref=buf.at[1, span],
            send_sem=relay_send.at[group], recv_sem=relay_recv.at[group],
            device_id=partner, device_id_type=MESH,
        )

    def meta_copy(ref, ref_there, number, target):
        return pltpu.make_async_remote_copy(
            src_ref=ref, dst_ref=ref_there, send_sem=meta_send.at[number], recv_sem=meta_recv.at[number],
            device_id=target, device_id_type=MESH,
        )

    mine = meta.at[y, z, x * 2 + core]
    stages = [
        [meta_copy(pos_ref, mine, number, target) for number, (target, unused) in enumerate(line)],
        [meta_copy(meta.at[y, z], meta.at[y, z], 7 + i, t) for i, (t, unused) in enumerate(column)],
        [meta_copy(meta.at[y], meta.at[y], 10 + i, t) for i, (t, unused) in enumerate(plane)],
    ]

    edges(0, lambda copy: copy.start())
    for copy in stages[0]:
        copy.start()
    own.wait()
    own_meta.wait()

    rows_id[...] = (lax.broadcasted_iota(jnp.int32, (512, 128), 0) - 256).astype(jnp.float32).astype(jnp.bfloat16)
    acc[...] = jnp.zeros_like(acc)
    for index, source in enumerate((load_ref, thick_ref)):
        pltpu.make_async_copy(source, wraw.at[index], w_sem.at[index]).wait()

    def order_weights(first, last):
        @pl.loop(first, last)
        def _(d):
            span = pl.ds(pl.multiple_of(d * 256, 256), 256)
            both = jnp.concatenate([wraw[0, span, :], wraw[1, span, :]], axis=1)
            moved = jnp.dot(permt_ref[...], both, preferred_element_type=jnp.float32).astype(jnp.bfloat16)
            place = pl.ds(pl.multiple_of(d * 16, 16), 16)
            for g in range(2 * CHUNKS):
                wperm[g, 0, place, :] = moved[g * 16 : (g + 1) * 16, :128]
                wperm[g, 1, place, :] = moved[g * 16 : (g + 1) * 16, 128:]

    def turn_weights(first, last):
        @pl.loop(first, last)
        def _(g):
            for index in range(2):
                wt[g, :, index * 512 : (index + 1) * 512] = wperm[g, index].T

    lane = lax.broadcasted_iota(jnp.int32, (32, 128), 1)

    def chunk(m, side):
        for i in range(CHUNK):
            sx, sy, sz = source_of(m * CHUNK + i)
            source_core = core if side == 0 else 1 - core
            pos = meta[sy, sz, sx * 2 + source_core]
            q = pos - 64.0 * p.astype(jnp.float32)
            inside = jnp.logical_and(q > -0.5, q < 63.5)
            target = jnp.where(inside, q * 8.0 + (i - 256.0), 1000.0).astype(jnp.bfloat16)
            onehot[:, i * 128 : (i + 1) * 128] = jnp.where(
                rows_id[...] == target, jnp.ones((), jnp.bfloat16), jnp.zeros((), jnp.bfloat16)
            )
        raw = buf[side, m * CHUNK : (m + 1) * CHUNK].reshape(CHUNK * 128, 256)
        sel[...] = jnp.dot(onehot[...], raw, preferred_element_type=jnp.float32)
        for b in range(16):
            delay = delay_ref[b, 0]
            keep = lane >= delay
            for index in range(2):
                piece = sel[b * 32 : (b + 1) * 32, index * 128 : (index + 1) * 128]
                piece = jnp.where(keep, pltpu.roll(piece, delay, 1), 0.0)
                shifted[index * 512 + b * 32 : index * 512 + (b + 1) * 32, :] = piece.astype(jnp.bfloat16)
        acc[...] += jnp.dot(wt[side * CHUNKS + m], shifted[...], preferred_element_type=jnp.float32)

    order_weights(0, 16)
    pending = []
    done_relays = set()

    def work(item):
        m, side = item
        if side == 1:
            for group in range(m * CHUNK // RELAY, (m + 1) * CHUNK // RELAY):
                relay(group).wait_recv()
        chunk(m, side)

    for n in range(1, CHIPS):
        arrival(n).wait_recv()
        edges(n, lambda copy: copy.start())
        if n % RELAY == RELAY - 1:
            relay(n // RELAY).start()
        if n == 6:
            for copy in stages[0]:
                copy.wait_recv()
            for copy in stages[1]:
                copy.start()
            order_weights(16, 32)
        if n == 21:
            for copy in stages[1]:
                copy.wait_recv()
            for copy in stages[2]:
                copy.start()
        if n in (12, 16):
            turn_weights(0 if n == 12 else 8, 8 if n == 12 else 16)
        if n % CHUNK == CHUNK - 1:
            pending.append((n // CHUNK, 0))
            if n // CHUNK > 0:
                pending.append((n // CHUNK - 1, 1))
        if n == 31:
            for copy in stages[2]:
                copy.wait_recv()
        if n >= 32 and n % 3 == 0 and pending:
            work(pending.pop(0))
    pending.append((CHUNKS - 1, 1))
    for item in pending:
        work(item)

    part[...] = acc[...].T
    shares = []
    for step in range(1, 4):
        there = lax.rem(p + step, 4)
        shares.append(
            pltpu.make_async_remote_copy(
                src_ref=part.at[pl.ds(pl.multiple_of(there * 32, 32), 32), :],
                dst_ref=arrived.at[step - 1],
                send_sem=rs_send.at[step - 1],
                recv_sem=rs_recv.at[step - 1],
                device_id=(there, o),
                device_id_type=MESH,
            )
        )
    for copy in shares:
        copy.start()
    total = part[pl.ds(pl.multiple_of(p * 32, 32), 32), :]
    for n in range(CHIPS):
        edges(n, lambda copy: copy.wait_send())
    for group in range(CHIPS // RELAY):
        relay(group).wait_send()
    for stage in stages:
        for copy in stage:
            copy.wait_send()
    for copy in shares:
        copy.wait()
    out_ref[...] = total + arrived[0] + arrived[1] + arrived[2]


def per_device(les_rows, les_dest, loading_weight, thickness_weight, delays):
    p = lax.axis_index("panel")
    o = lax.axis_index("obs")
    velocity = jnp.pad(les_rows[:, 1, :].astype(jnp.float32), ((0, 0), (1, 1)))
    rate = ((velocity[:, 2:] - velocity[:, :-2]) * 0.5).astype(jnp.bfloat16)
    blk = jnp.concatenate([les_rows[:, 0, :], rate], axis=1)
    dest = les_dest[:, 0]
    row = jnp.arange(dest.shape[0], dtype=jnp.int32)
    same = jnp.logical_and(dest[:, None] == dest[None, :], row[:, None] < row[None, :])
    rank = jnp.sum(same.astype(jnp.int32), axis=0)
    pos = (dest * 2 + rank).astype(jnp.float32).reshape(1, -1)

    x = lax.rem(o, 2) * 2 + p // 2
    core = lax.rem(p, 2)
    index = np.arange(256)
    side, m, cap, i = index // 128, index // 16 % 8, index // 8 % 2, index % 8
    offsets = np.array(OFFSETS)[m * CHUNK + i]
    sx = lax.rem(x + jnp.asarray(4 - offsets[:, 0], jnp.int32), 4)
    sy = lax.rem(o // 8 + jnp.asarray(4 - offsets[:, 1], jnp.int32), 4)
    sz = lax.rem(lax.rem(o // 2, 4) + jnp.asarray(4 - offsets[:, 2], jnp.int32), 4)
    sc = lax.rem(core + jnp.asarray(side, jnp.int32), 2)
    owner = (lax.rem(sx, 2) * 2 + sc) * 32 + sy * 8 + sz * 2 + sx // 2
    want = owner * 2 + jnp.asarray(cap, jnp.int32)
    permt = (want[:, None] == jnp.arange(256, dtype=jnp.int32)[None, :]).astype(jnp.bfloat16)

    vmem = pl.BlockSpec(memory_space=pltpu.VMEM)
    return pl.pallas_call(
        kernel,
        out_shape=jax.ShapeDtypeStruct((32, 128), jnp.float32),
        in_specs=[vmem, vmem, vmem, pl.BlockSpec(memory_space=pl.ANY), pl.BlockSpec(memory_space=pl.ANY),
                  pl.BlockSpec(memory_space=pltpu.SMEM)],
        out_specs=vmem,
        scratch_shapes=[
            pltpu.VMEM((2, CHIPS, 128, 256), jnp.bfloat16),
            pltpu.VMEM((4, 4, 8, 1, 128), jnp.float32),
            pltpu.VMEM((2, 8192, 128), jnp.bfloat16),
            pltpu.VMEM((2 * CHUNKS, 2, 512, 128), jnp.bfloat16),
            pltpu.VMEM((2 * CHUNKS, 128, 1024), jnp.bfloat16),
            pltpu.VMEM((512, 1024), jnp.bfloat16),
            pltpu.VMEM((512, 128), jnp.bfloat16),
            pltpu.VMEM((512, 256), jnp.float32),
            pltpu.VMEM((1024, 128), jnp.bfloat16),
            pltpu.VMEM((128, 128), jnp.float32),
            pltpu.VMEM((128, 128), jnp.float32),
            pltpu.VMEM((3, 32, 128), jnp.float32),
            pltpu.SemaphoreType.DMA((len(EDGES),)),
            pltpu.SemaphoreType.DMA((CHIPS,)),
            pltpu.SemaphoreType.DMA((CHIPS // RELAY,)),
            pltpu.SemaphoreType.DMA((CHIPS // RELAY,)),
            pltpu.SemaphoreType.DMA((13,)),
            pltpu.SemaphoreType.DMA((13,)),
            pltpu.SemaphoreType.DMA((2,)),
            pltpu.SemaphoreType.DMA((2,)),
            pltpu.SemaphoreType.DMA((3,)),
            pltpu.SemaphoreType.DMA((3,)),
        ],
        compiler_params=pltpu.CompilerParams(collective_id=0, has_side_effects=True, vmem_limit_bytes=48 << 20),
    )(blk, pos, permt, loading_weight, thickness_weight, delays)


def solution(mesh):
    placed = (
        P(("panel", "obs"), None, None),
        P(("panel", "obs"), None),
        P("panel", "obs"),
        P("panel", "obs"),
        P("panel", "obs"),
    )
    return jax.shard_map(
        per_device, mesh=mesh, in_specs=placed, out_specs=P("panel", "obs"), check_vma=False
    )
```

```python
import itertools

import jax
import jax.numpy as jnp
import numpy as np
from jax import lax
from jax.experimental import pallas as pl
from jax.experimental.pallas import tpu as pltpu
from jax.sharding import PartitionSpec as P

MESH = pl.DeviceIdType.MESH
RING = 4
CHIPS = RING**3
CHUNK = 4
CHUNKS = CHIPS // CHUNK
ROWS = (48, 48, 32)
FIRST = (0, 48, 96)

STAGE1 = [(h, 0, 0, s) for s in (1, 3, 2) for h in range(3)]
STAGE2 = [(h, 0, s, None) for s in (1, 3, 2) for h in range(3)]
STAGE3 = [(h, s, g, None) for g, s in (
    (0, 1), (0, 3), (0, 2), (1, 1), (1, 3), (3, 1), (3, 3), (2, 1), (2, 3), (1, 2), (3, 2), (2, 2),
) for h in range(3)]
ARRIVALS = STAGE1 + STAGE2[:6] + STAGE3[:6] + STAGE2[6:] + STAGE3[6:]
NUMBER = {item: i for i, item in enumerate(ARRIVALS)}
GROUPS = [(h, 0, 0, None) for h in range(3)] + ARRIVALS[9:]
GROUP = {item: i for i, item in enumerate(GROUPS)}


def copies_after(item):
    h, o3, o2, o1 = item
    second, third = (h + 1) % 3, (h + 2) % 3
    if o1 is not None:
        return []
    if o3 == 0:
        found = [((h, 0, s, None), second, s) for s in (1, 3, 2)] if o2 == 0 else []
        return found + [((h, s, o2, None), third, s) for s in (1, 3)]
    turn = 1 if o2 % 2 == 0 else 3
    return [((h, 2, o2, None), third, turn)] if o3 == turn else []


def group_of(offset, h):
    return (h, offset[(h + 2) % 3], offset[(h + 1) % 3], None)


OFFSETS = sorted(
    itertools.product(range(RING), repeat=3), key=lambda o: (max(GROUP[group_of(o, h)] for h in range(3)), o)
)
READY = [max(GROUP[group_of(o, h)] for o in OFFSETS[m * CHUNK : (m + 1) * CHUNK] for h in range(3)) for m in range(CHUNKS)]


def kernel(
    blk_ref, code_ref, dest_ref, load_ref, thick_ref, delay_ref, out_ref,
    buf0, buf1, buf2, meta, pos, codes, dest, delays, permt, wraw, wperm, wt, onehot, sel, shifted, acc, part, arrived,
    own_sem, send1, recv1, relay_send, relay_recv, meta_send, meta_recv, rs_send, rs_recv,
):
    bufs = (buf0, buf1, buf2)
    p = lax.axis_index("panel")
    o = lax.axis_index("obs")
    x_lo, core = p // 2, lax.rem(p, 2)
    y, z, x_hi = o // 8, lax.rem(o // 2, 4), lax.rem(o, 2)
    x = x_hi * 2 + x_lo

    def device(cx, cy, cz, cc):
        return (lax.rem(cx, 2) * 2 + cc, cy * 8 + cz * 2 + cx // 2)

    line = [device(lax.rem(x + s, RING), y, z, core) for s in range(1, 4)]
    line += [device(lax.rem(x + s, RING), y, z, 1 - core) for s in range(0, 4)]
    column = [device(x, y, lax.rem(z + s, RING), core) for s in range(1, 4)]
    plane = [device(x, lax.rem(y + s, RING), z, core) for s in range(1, 4)]
    partner = line[3]
    first = core == 0

    def pick(a, b):
        return tuple(jnp.where(first, u, v) for u, v in zip(a, b))

    near = {}
    for s in range(1, 4):
        near[(0, s)] = pick(line[s - 1], plane[s - 1])
        near[(1, s)] = pick(plane[s - 1], column[s - 1])
        near[(2, s)] = pick(column[s - 1], line[s - 1])

    turned = ((x, y, z), (y, z, x))
    back = []
    for side in range(2):
        mine = pick(turned[side], turned[1 - side])
        back.append([[lax.rem(mine[i] + (RING - v), RING) for v in range(RING)] for i in range(3)])

    local = [
        pltpu.make_async_copy(load_ref, wraw.at[0], own_sem.at[0]),
        pltpu.make_async_copy(thick_ref, wraw.at[1], own_sem.at[1]),
        pltpu.make_async_copy(code_ref, codes, own_sem.at[2]),
        pltpu.make_async_copy(dest_ref, dest, own_sem.at[3]),
        pltpu.make_async_copy(delay_ref, delays, own_sem.at[4]),
    ]
    for copy in (local[3], local[2], local[0], local[1], local[4]):
        copy.start()
    own = [
        pltpu.make_async_copy(blk_ref.at[pl.ds(FIRST[h], ROWS[h])], bufs[h].at[0, 0], own_sem.at[5 + h]) for h in range(3)
    ]
    for copy in own:
        copy.start()

    barrier = pltpu.get_barrier_semaphore()
    for target in line + column + plane:
        pl.semaphore_signal(barrier, inc=1, device_id=target, device_id_type=MESH)
    pl.semaphore_wait(barrier, 13)

    def span(item):
        h, o3, o2, o1 = item
        at = (o3 * RING + o2) * RING
        return bufs[h], (pl.ds(at, RING) if o1 is None else at + o1)

    def remote(source, item, target):
        ref, where = span(item)
        return pltpu.make_async_remote_copy(
            src_ref=source, dst_ref=ref.at[0, where], send_sem=send1.at[NUMBER[item]], recv_sem=recv1.at[NUMBER[item]],
            device_id=target, device_id_type=MESH,
        )

    def arrival(item):
        ref, where = span(item)
        return remote(ref.at[0, where], item, partner)

    sent = []

    def send(source, item, axis, step):
        copy = remote(source, item, near[(axis, step)])
        copy.start()
        sent.append(copy)

    def forward(item):
        ref, where = span(item)
        for landed, axis, step in copies_after(item):
            send(ref.at[0, where], landed, axis, step)
        relay(item).start()

    def relay(item):
        ref, where = span(item)
        return pltpu.make_async_remote_copy(
            src_ref=ref.at[0, where], dst_ref=ref.at[1, where],
            send_sem=relay_send.at[GROUP[item]], recv_sem=relay_recv.at[GROUP[item]],
            device_id=partner, device_id_type=MESH,
        )

    for s in (1, 3, 2):
        for h in range(3):
            send(blk_ref.at[pl.ds(FIRST[h], ROWS[h])], (h, 0, 0, s), h, s)

    local[3].wait()
    here = jnp.broadcast_to(dest[...], (128, 128)).astype(jnp.float32)
    there = here.T
    earlier = lax.broadcasted_iota(jnp.int32, (128, 128), 0) < lax.broadcasted_iota(jnp.int32, (128, 128), 1)
    same = jnp.where(jnp.logical_and(here == there, earlier), 1.0, 0.0)
    pos[...] = there[0:1, :] * 2.0 + jnp.sum(same, axis=0, keepdims=True)

    local[2].wait()
    for side in range(2):
        code = codes[side * 128 : (side + 1) * 128, :]
        along = []
        for i in range(3):
            digit = lax.rem(code // (RING**i), RING)
            value = jnp.zeros_like(digit)
            for v in range(RING):
                value = jnp.where(digit == v, back[side][i][v], value)
            along.append(value)
        straight = first if side == 0 else jnp.logical_not(first)
        sx, sy, sz = (jnp.where(straight, along[a], along[b]) for a, b in ((0, 2), (1, 0), (2, 1)))
        source_core = core if side == 0 else 1 - core
        owner = (lax.rem(sx, 2) * 2 + source_core) * 32 + sy * 8 + sz * 2 + sx // 2
        want = owner * 2 + code // CHIPS
        for half in range(2):
            column_id = lax.broadcasted_iota(jnp.int32, (128, 128), 1) + half * 128
            permt[side * 128 : (side + 1) * 128, half * 128 : (half + 1) * 128] = jnp.where(
                want == column_id, 1.0, 0.0
            ).astype(jnp.bfloat16)

    own_meta = pltpu.make_async_copy(pos, meta.at[y * 32 + z * 8 + x * 2 + core], own_sem.at[8])
    own_meta.start()
    for copy in own:
        copy.wait()
    for index in range(2):
        local[index].wait()

    def order_weights(start, stop):
        @pl.loop(start, stop)
        def _(d):
            rows = pl.ds(pl.multiple_of(d * 256, 256), 256)
            both = jnp.concatenate([wraw[0, rows, :], wraw[1, rows, :]], axis=1)
            moved = jnp.dot(permt[...], both, preferred_element_type=jnp.float32)
            place = pl.ds(pl.multiple_of(d * 8, 8), 8)
            for g in range(2 * CHUNKS):
                wperm[g, 0, place, :] = moved[g * 8 : (g + 1) * 8, :128]
                wperm[g, 1, place, :] = moved[g * 8 : (g + 1) * 8, 128:]

    def turn_weights(start, stop):
        @pl.loop(start, stop)
        def _(g):
            for index in range(2):
                wt[g, :, index * 256 : (index + 1) * 256] = wperm[g, index].astype(jnp.bfloat16).T

    lane = lax.broadcasted_iota(jnp.int32, (16, 128), 1)
    row_id = lax.broadcasted_iota(jnp.int32, (256, 128), 0).astype(jnp.float32).astype(jnp.bfloat16)
    group_first = 64.0 * p.astype(jnp.float32)
    one, nil = jnp.ones((), jnp.bfloat16), jnp.zeros((), jnp.bfloat16)
    weights = ((2, 32, 8), (32, 8, 2))
    index_of = []
    for side in range(2):
        scale = pick(weights[side], weights[1 - side])
        source_core = core if side == 0 else 1 - core
        index_of.append(
            [[back[side][i][v] * scale[i] + (source_core if i == 0 else 0) for v in range(RING)] for i in range(3)]
        )

    def chunk(m, side):
        pieces = []
        for i in range(CHUNK):
            offset = OFFSETS[m * CHUNK + i]
            tab = index_of[side]
            q = meta[tab[0][offset[0]] + tab[1][offset[1]] + tab[2][offset[2]]] - group_first
            inside = jnp.logical_and(q > -0.5, q < 63.5)
            target = jnp.where(inside, q * float(CHUNK) + float(i), 1000.0).astype(jnp.bfloat16)
            onehot[:, i * 128 : (i + 1) * 128] = jnp.where(row_id == target, one, nil)
            for h in range(3):
                unused, o3, o2, unused = group_of(offset, h)
                pieces.append(bufs[h][side, (o3 * RING + o2) * RING + offset[h]])
        raw = jnp.concatenate(pieces, axis=0)
        sel[...] = jnp.dot(onehot[...], raw, preferred_element_type=jnp.float32)
        for b in range(16):
            delay = delays[b, 0]
            keep = lane >= delay
            for index in range(2):
                piece = sel[b * 16 : (b + 1) * 16, index * 128 : (index + 1) * 128]
                piece = jnp.where(keep, pltpu.roll(piece, delay, 1), 0.0)
                shifted[index * 256 + b * 16 : index * 256 + (b + 1) * 16, :] = piece.astype(jnp.bfloat16)
        acc[...] += jnp.dot(wt[side * CHUNKS + m], shifted[...], preferred_element_type=jnp.float32)

    def meta_copy(ref, ref_there, number, target):
        return pltpu.make_async_remote_copy(
            src_ref=ref, dst_ref=ref_there, send_sem=meta_send.at[number], recv_sem=meta_recv.at[number],
            device_id=target, device_id_type=MESH,
        )

    mine = meta.at[y * 32 + z * 8 + x * 2 + core]
    ring_z = meta.at[pl.ds(y * 32 + z * 8, 8)]
    ring_y = meta.at[pl.ds(y * 32, 32)]
    stages = [
        [meta_copy(pos, mine, number, target) for number, target in enumerate(line)],
        [meta_copy(ring_z, ring_z, 7 + i, target) for i, target in enumerate(column)],
        [meta_copy(ring_y, ring_y, 10 + i, target) for i, target in enumerate(plane)],
    ]

    acc[...] = jnp.zeros_like(acc)
    order_weights(0, 4)
    own_meta.wait()
    for copy in stages[0]:
        copy.start()
    order_weights(4, 8)
    local[4].wait()

    todo = []
    relayed = set()

    def work(item):
        unused, m, side = item
        if side == 1:
            needed = sorted({GROUP[group_of(offset, h)] for offset in OFFSETS[m * CHUNK : (m + 1) * CHUNK] for h in range(3)})
            for g in needed:
                if g not in relayed:
                    relayed.add(g)
                    relay(GROUPS[g]).wait_recv()
        chunk(m, side)

    for item in STAGE1:
        arrival(item).wait_recv()
    for h in range(3):
        forward((h, 0, 0, None))
    for copy in stages[0]:
        copy.wait_recv()
    for copy in stages[1]:
        copy.start()
    order_weights(8, 28)
    for copy in stages[1]:
        copy.wait_recv()
    for copy in stages[2]:
        copy.start()
    late = len(GROUPS)
    for m in range(CHUNKS):
        todo.append((READY[m], m, 0))
        todo.append((READY[m] + LAG, m, 1))
    todo.sort()
    for item in ARRIVALS[9:]:
        arrival(item).wait_recv()
        forward(item)
        now = GROUP[item]
        if item == STAGE2[5]:
            order_weights(28, 32)
            turn_weights(0, 8)
        if item == STAGE3[5]:
            turn_weights(8, 32)
            for copy in stages[2]:
                copy.wait_recv()
        if now >= GROUP[STAGE3[5]]:
            for unused in range(2):
                if todo and todo[0][0] <= now:
                    work(todo.pop(0))
    for item in todo:
        work(item)

    part[...] = acc[...].T
    shares = []
    for step in range(1, 4):
        place = lax.rem(p + step, 4)
        shares.append(
            pltpu.make_async_remote_copy(
                src_ref=part.at[pl.ds(pl.multiple_of(place * 32, 32), 32), :],
                dst_ref=arrived.at[step - 1],
                send_sem=rs_send.at[step - 1],
                recv_sem=rs_recv.at[step - 1],
                device_id=(place, o),
                device_id_type=MESH,
            )
        )
    for copy in shares:
        copy.start()
    total = part[pl.ds(pl.multiple_of(p * 32, 32), 32), :]
    for copy in sent:
        copy.wait_send()
    for item in GROUPS:
        relay(item).wait_send()
    for stage in stages:
        for copy in stage:
            copy.wait_send()
    for copy in shares:
        copy.wait()
    out_ref[...] = total + arrived[0] + arrived[1] + arrived[2]


LAG = 4


def per_device(les_rows, les_dest, loading_weight, thickness_weight, delays):
    velocity = jnp.pad(les_rows[:, 1, :].astype(jnp.float32), ((0, 0), (1, 1)))
    rate = ((velocity[:, 2:] - velocity[:, :-2]) * 0.5).astype(jnp.bfloat16)
    blk = jnp.concatenate([les_rows[:, 0, :], rate], axis=1)

    index = np.arange(256)
    m, cap, i = index // 8 % CHUNKS, index // CHUNK % 2, index % CHUNK
    offsets = np.array(OFFSETS)[m * CHUNK + i]
    code = offsets @ np.array([1, RING, RING**2]) + CHIPS * cap
    code = jnp.asarray(np.repeat(code[:, None], 128, axis=1), jnp.int32)

    vmem = pl.BlockSpec(memory_space=pltpu.VMEM)
    hbm = pl.BlockSpec(memory_space=pltpu.HBM)
    return pl.pallas_call(
        kernel,
        out_shape=jax.ShapeDtypeStruct((32, 128), jnp.float32),
        in_specs=[vmem, hbm, hbm, hbm, hbm, hbm],
        out_specs=vmem,
        scratch_shapes=[
            pltpu.VMEM((2, CHIPS, ROWS[0], 256), jnp.bfloat16),
            pltpu.VMEM((2, CHIPS, ROWS[1], 256), jnp.bfloat16),
            pltpu.VMEM((2, CHIPS, ROWS[2], 256), jnp.bfloat16),
            pltpu.VMEM((128, 1, 128), jnp.float32),
            pltpu.VMEM((1, 128), jnp.float32),
            pltpu.VMEM((256, 128), jnp.int32),
            pltpu.VMEM((128, 1), jnp.int32),
            pltpu.SMEM((16, 1), jnp.int32),
            pltpu.VMEM((256, 256), jnp.bfloat16),
            pltpu.VMEM((2, 8192, 128), jnp.bfloat16),
            pltpu.VMEM((2 * CHUNKS, 2, 256, 128), jnp.float32),
            pltpu.VMEM((2 * CHUNKS, 128, 512), jnp.bfloat16),
            pltpu.VMEM((256, 512), jnp.bfloat16),
            pltpu.VMEM((256, 256), jnp.float32),
            pltpu.VMEM((512, 128), jnp.bfloat16),
            pltpu.VMEM((128, 128), jnp.float32),
            pltpu.VMEM((128, 128), jnp.float32),
            pltpu.VMEM((3, 32, 128), jnp.float32),
            pltpu.SemaphoreType.DMA((9,)),
            pltpu.SemaphoreType.DMA((len(ARRIVALS),)),
            pltpu.SemaphoreType.DMA((len(ARRIVALS),)),
            pltpu.SemaphoreType.DMA((len(GROUPS),)),
            pltpu.SemaphoreType.DMA((len(GROUPS),)),
            pltpu.SemaphoreType.DMA((13,)),
            pltpu.SemaphoreType.DMA((13,)),
            pltpu.SemaphoreType.DMA((3,)),
            pltpu.SemaphoreType.DMA((3,)),
        ],
        compiler_params=pltpu.CompilerParams(collective_id=0, has_side_effects=True, vmem_limit_bytes=60 << 20),
    )(blk, code, les_dest, loading_weight, thickness_weight, delays)


def solution(mesh):
    placed = (
        P(("panel", "obs"), None, None),
        P(("panel", "obs"), None),
        P("panel", "obs"),
        P("panel", "obs"),
        P("panel", "obs"),
    )
    return jax.shard_map(
        per_device, mesh=mesh, in_specs=placed, out_specs=P("panel", "obs"), check_vma=False
    )
```
